128 devices in a mesh: row: 16 (over x, z), col: 8 (over y, core).
Axes of the slice: x: 4, y: 4, z: 4, core: 2. Of those that a mesh axis runs over, the one named last changes fastest.
Arguments:
- amplitudes: bfloat16 [16384, 16384], P('row', 'col'), may hold values from -6 to 6
- integrals: bfloat16 [16384, 4096], P('col', 'row'), may hold values from -0.046875 to 0.046875
- amp_mask: int32 [128, 128], P('row', 'col'), may hold values 0 or 1
- int_mask: int32 [128, 32], P('col', 'row'), may hold values 0 or 1
Outputs:
- ladder: bfloat16 [16384, 4096], P('row', 'col')
The draws below stay inside these ranges and needn't reach their ends.
All inputs are finite; a program needn't handle non-finite values. No bound on the sum of `amp_mask` or of `int_mask` on one device may be relied on, other than what follows from the above.
Results may differ from the reference program's by a relative error of at most 0.001.
Values may be sent and summed in bfloat16 or wider, within the bound.
A program may use at most 128 MiB of HBM per device.

```python
import jax
import jax.numpy as jnp

TILE = 128
PAIRS = 16384
CONTR = 16384
COLS = 4096


def touch_ends(array, rng, least, top_value):
    longest = array.shape.index(max(array.shape))
    spots = []
    for shift in (0, 1):
        where = [jax.random.randint(jax.random.fold_in(rng, axis), (), 0, length) for axis, length in enumerate(array.shape)]
        where[longest] = (where[longest] + shift) % array.shape[longest]
        spots.append(tuple(where))
    return array.at[spots[0]].set(least).at[spots[1]].set(top_value)


def shard_levels(rng, dims, split, smallest, top_value):
    def one(axis_at, shards_of):
        draws = jax.random.uniform(jax.random.fold_in(jax.random.fold_in(rng, 6), axis_at), (shards_of,), jnp.float32, smallest / len(split), top_value / len(split))
        return jnp.repeat(jnp.exp(draws), dims[axis_at] // shards_of).reshape((-1,) + (1,) * (len(dims) - axis_at - 1))

    gain = one(*split[0])
    for cut in split[1:]:
        gain = gain * one(*cut)
    return gain


def noise(own_key, extent, scale, reach, pieces=(), held_as=jnp.bfloat16):
    result = scale * jax.random.normal(own_key, extent, jnp.float32)
    if pieces:
        result = result * shard_levels(own_key, extent, pieces, -0.22, 0.18)
    return jnp.clip(result, -reach, reach).astype(held_as)


def setup_inputs(seed: int = 0) -> dict:
    arg_keys = jax.random.split(jax.random.key(seed), 5)
    return {
        "amplitudes": noise(arg_keys[0], (PAIRS, CONTR), 1.0, 6.0, ((0, 16), (1, 8))),
        "integrals": noise(arg_keys[1], (CONTR, COLS), CONTR ** -0.5, 0.046875, ((0, 8), (1, 16))),
        "amp_mask": touch_ends((jax.random.randint(arg_keys[2], (PAIRS // TILE, CONTR // TILE), 0, 2) < 1).astype(jnp.int32), jax.random.fold_in(arg_keys[2], 1), 0, 1),
        "int_mask": touch_ends((jax.random.randint(arg_keys[3], (CONTR // TILE, COLS // TILE), 0, 2) < 1).astype(jnp.int32), jax.random.fold_in(arg_keys[3], 1), 0, 1),
    }


def expand(mask):
    spread = jnp.repeat(jnp.repeat(mask, TILE, axis=0), TILE, axis=1)
    return spread.astype(jnp.bfloat16)


def reference(amplitudes, integrals, amp_mask, int_mask):
    sparse_amp = amplitudes * expand(amp_mask)
    sparse_int = integrals * expand(int_mask)
    ladder = jnp.dot(sparse_amp, sparse_int, preferred_element_type=jnp.float32)
    return ladder.astype(jnp.bfloat16)
```

```python
import jax
import jax.numpy as jnp
from jax import lax
from jax.experimental import pallas as pl
from jax.experimental.pallas import tpu as pltpu
from jax.sharding import PartitionSpec as P

MESH = pl.DeviceIdType.MESH
TILE = 128
ROWS = 1024
DEPTH = 2048
WIDE = 128
BLOCK = 256
STEP = (0, 3, 1, 2)


def kernel(
    a_hbm, b_hbm, am, im, o_hbm,
    a_buf, b_raw, b_out, b_buf, c_buf, near, mine, out_buf, out_send,
    load_sem, pair_s, pair_r, ring_s, ring_r, y_s, y_r, o_s, o_r, store_sem,
):
    r, q = lax.axis_index("row"), lax.axis_index("col")
    x, z, y, c = r // 4, r % 4, q // 2, q % 2

    def dev(x_, z_, y_, c_):
        return (x_ * 4 + z_, y_ * 2 + c_)

    sibling = dev(x, z, y, 1 - c)
    on_x, on_z = 1 - c, c

    def along_first(d):
        return dev((x + d * on_x) % 4, (z + d * on_z) % 4, y, c)

    def along_second(d):
        return dev((x + d * on_z) % 4, (z + d * on_x) % 4, y, c)

    def along_y(d):
        return dev(x, z, (y + d) % 4, c)

    started = []

    def send(src, dst, ss, rs, to):
        copy = pltpu.make_async_remote_copy(
            src_ref=src, dst_ref=dst, send_sem=ss, recv_sem=rs, device_id=to, device_id_type=MESH
        )
        copy.start()
        return copy

    def arrived(dst, rs):
        pltpu.make_async_remote_copy(
            src_ref=dst, dst_ref=dst, send_sem=rs, recv_sem=rs, device_id=sibling, device_id_type=MESH
        ).wait_recv()

    loads = [
        pltpu.make_async_copy(b_hbm.at[:, pl.ds(h * WIDE, WIDE)], b_raw.at[h], load_sem.at[h])
        for h in range(2)
    ] + [pltpu.make_async_copy(a_hbm, a_buf.at[c], load_sem.at[2])]
    for load in loads:
        load.start()

    barrier = pltpu.get_barrier_semaphore()
    peers = [sibling]
    for d in (1, 3):
        peers += [along_first(d), along_second(d), along_y(d)]
    for peer in peers:
        pl.semaphore_signal(barrier, inc=1, device_id=peer, device_id_type=MESH)

    loads[0].wait()
    loads[1].wait()

    def mask_b(t, carry):
        rows = pl.ds(pl.multiple_of(t * TILE, TILE), TILE)
        keep = im[t, 1 - c].astype(jnp.float32)
        b_out[rows, :] = (b_raw[1 - c, rows, :].astype(jnp.float32) * keep).astype(jnp.bfloat16)
        keep = im[t, c].astype(jnp.float32)
        b_buf[0, 0, c, rows, :] = (b_raw[c, rows, :].astype(jnp.float32) * keep).astype(jnp.bfloat16)
        return carry

    lax.fori_loop(0, DEPTH // TILE, mask_b, 0)
    pl.semaphore_wait(barrier, 7)

    def ring(i, j, h, ti, tj, direction, to):
        started.append(
            send(
                b_buf.at[i, j, h], b_buf.at[ti, tj, h],
                ring_s.at[i, j, h, direction], ring_r.at[ti, tj, h], to,
            )
        )

    def got(i, j, h):
        arrived(b_buf.at[i, j, h], ring_r.at[i, j, h])

    def first_out(h):
        ring(0, 0, h, 1, 0, 0, along_first(1))
        ring(0, 0, h, 2, 0, 1, along_first(3))

    def second_out(i, h):
        ring(i, 0, h, i, 1, 2, along_second(1))
        ring(i, 0, h, i, 2, 3, along_second(3))

    started.append(send(b_out, b_buf.at[0, 0, c], pair_s.at[0], pair_r.at[0], sibling))
    first_out(c)
    second_out(0, c)

    loads[2].wait()

    def mask_a(t, carry):
        rows = pl.ds(pl.multiple_of(t * TILE, TILE), TILE)
        for k in range(DEPTH // TILE):
            cols = pl.ds(k * TILE, TILE)
            keep = am[t, k].astype(jnp.float32)
            a_buf[c, rows, cols] = (a_buf[c, rows, cols].astype(jnp.float32) * keep).astype(jnp.bfloat16)
        return carry

    lax.fori_loop(0, ROWS // TILE, mask_a, 0)
    arrived(b_buf.at[0, 0, 1 - c], pair_r.at[0])
    first_out(1 - c)
    second_out(0, 1 - c)
    started.append(send(a_buf.at[c], a_buf.at[c], pair_s.at[1], pair_r.at[1], sibling))

    def first_forward():
        got(1, 0, 0)
        ring(1, 0, 0, 3, 0, 0, along_first(1))
        got(2, 0, 1)
        ring(2, 0, 1, 3, 0, 1, along_first(3))
        got(1, 0, 1)
        got(2, 0, 0)

    def second_forward(i):
        got(i, 1, 0)
        ring(i, 1, 0, i, 3, 2, along_second(1))
        got(i, 2, 1)
        ring(i, 2, 1, i, 3, 3, along_second(3))

    def second_rest(i):
        got(i, 1, 1)
        got(i, 2, 0)

    def product(*slots):
        def step(t, carry):
            rows = pl.ds(pl.multiple_of(t * BLOCK, BLOCK), BLOCK)
            total = None
            for h in range(2):
                units = [b_buf[i, j, h] for i, j in slots]
                unit = units[0] if len(units) == 1 else jnp.concatenate(units, axis=1)
                part = jnp.dot(a_buf[h, rows, :], unit, preferred_element_type=jnp.float32)
                total = part if total is None else total + part
            for n, (i, j) in enumerate(slots):
                c_buf[i * 4 + j, rows, :] = total[:, n * WIDE : (n + 1) * WIDE]
            return carry

        lax.fori_loop(0, ROWS // BLOCK, step, 0)

    def place(i, j):
        di, dj = STEP[i], STEP[j]
        return (x + di * on_x + dj * on_z) % 4, (z + di * on_z + dj * on_x) % 4

    HALF = ROWS // 2

    def half(n):
        return pl.ds(n * HALF, HALF)

    def y_copy(u, n, dst, ss, rs, to):
        return pltpu.make_async_remote_copy(
            src_ref=c_buf.at[u, half(n)], dst_ref=dst, send_sem=ss, recv_sem=rs, device_id=to, device_id_type=MESH
        )

    def far_copy(u, n, zz):
        return y_copy(u, n, near.at[n, zz], y_s.at[u, n], y_r.at[n, zz], along_y(3 if n == 0 else 1))

    def near_copy(u, n, side, zz):
        return y_copy(
            u, n, mine.at[side, zz, half(n)], y_s.at[u, n], y_r.at[2 + side * 2 + n, zz], along_y(3 if side == 0 else 1)
        )

    def pass_on(i, j):
        u = i * 4 + j
        xx, zz = place(i, j)
        role = (y - xx + 4) % 4

        @pl.when(role == 2)
        def _():
            far_copy(u, 0, zz).start()
            far_copy(u, 1, zz).start()

        @pl.when(role == 1)
        def _():
            near_copy(u, 1, 0, zz).start()

        @pl.when(role == 3)
        def _():
            near_copy(u, 0, 1, zz).start()

    def add_on(i, j):
        u = i * 4 + j
        xx, zz = place(i, j)
        role = (y - xx + 4) % 4

        def add(n, side):
            arrived(near.at[n, zz], y_r.at[n, zz])
            c_buf[u, half(n), :] = c_buf[u, half(n), :] + near[n, zz]
            near_copy(u, n, side, zz).start()

        @pl.when(role == 1)
        def _():
            add(0, 0)

        @pl.when(role == 3)
        def _():
            add(1, 1)

    waiting = []

    def run(*slots):
        product(*slots)
        for i, j in slots:
            pass_on(i, j)
        for i, j in waiting:
            add_on(i, j)
        waiting[:] = slots

    arrived(a_buf.at[1 - c], pair_r.at[1])
    run((0, 0))
    first_forward()
    for h in range(2):
        second_out(1, h)
    second_forward(0)
    for h in range(2):
        second_out(2, h)
    run((1, 0), (2, 0))
    second_rest(0)
    run((0, 1), (0, 2))
    got(3, 0, 0)
    got(3, 0, 1)
    for h in range(2):
        second_out(3, h)
    got(0, 3, 0)
    got(0, 3, 1)
    second_forward(1)
    run((3, 0), (0, 3))
    second_rest(1)
    run((1, 1), (1, 2))
    second_forward(2)
    second_rest(2)
    run((2, 1), (2, 2))
    second_forward(3)
    for i in (1, 2):
        got(i, 3, 0)
        got(i, 3, 1)
    run((1, 3), (2, 3))
    second_rest(3)
    run((3, 1), (3, 2))
    got(3, 3, 0)
    got(3, 3, 1)
    run((3, 3))
    for i, j in waiting:
        add_on(i, j)

    ahead = (y - x + 4) % 4
    slot = (ahead == 1) * 2 + (ahead == 2) * 3 + (ahead == 3) * 1

    def own(j):
        u = jnp.where(c == 0, slot * 4 + j, j * 4 + slot)
        zz = (z + STEP[j]) % 4
        return u, zz

    def store(n):
        return pltpu.make_async_copy(
            out_buf.at[n], o_hbm.at[:, pl.ds(n * WIDE, WIDE)], store_sem.at[n]
        )

    for j in range(4):
        u, zz = own(j)
        for side in range(2):
            for n in range(2):
                arrived(mine.at[side, zz, half(n)], y_r.at[2 + side * 2 + n, zz])
        spot = (zz % 2) * 2 + c
        stays = zz // 2 == c

        def value(t):
            rows = pl.ds(pl.multiple_of(t * TILE, TILE), TILE)
            return rows, (c_buf[u, rows, :] + (mine[0, zz, rows, :] + mine[1, zz, rows, :])).astype(jnp.bfloat16)

        @pl.when(stays)
        def _():
            def step(t, carry):
                rows, v = value(t)
                out_buf[spot, rows, :] = v
                return carry

            lax.fori_loop(0, ROWS // TILE, step, 0)

        @pl.when(jnp.logical_not(stays))
        def _():
            def step(t, carry):
                rows, v = value(t)
                out_send[zz % 2, rows, :] = v
                return carry

            lax.fori_loop(0, ROWS // TILE, step, 0)
            send(out_send.at[zz % 2], out_buf.at[spot], o_s.at[zz % 2], o_r.at[zz % 2], sibling)

    for n in range(2):
        arrived(out_buf.at[n * 2 + 1 - c], o_r.at[n])
    for n in range(4):
        store(n).start()

    for copy in started:
        copy.wait_send()
    for u in range(16):
        i, j = u // 4, u % 4
        xx, zz = place(i, j)
        role = (y - xx + 4) % 4

        @pl.when(role != 0)
        def _():
            for n in range(2):
                far_copy(u, n, zz).wait_send()

    for n in range(2):
        pltpu.make_async_remote_copy(
            src_ref=out_send.at[n], dst_ref=out_send.at[n], send_sem=o_s.at[n], recv_sem=o_s.at[n],
            device_id=sibling, device_id_type=MESH,
        ).wait_send()
    for n in range(4):
        store(n).wait()


def per_device(amplitudes, integrals, amp_mask, int_mask):
    bf16, f32 = jnp.bfloat16, jnp.float32
    dma = pltpu.SemaphoreType.DMA
    return pl.pallas_call(
        kernel,
        out_shape=jax.ShapeDtypeStruct((ROWS, 4 * WIDE), bf16),
        in_specs=[
            pl.BlockSpec(memory_space=pl.ANY),
            pl.BlockSpec(memory_space=pl.ANY),
            pl.BlockSpec(memory_space=pltpu.SMEM),
            pl.BlockSpec(memory_space=pltpu.SMEM),
        ],
        out_specs=pl.BlockSpec(memory_space=pl.ANY),
        scratch_shapes=[
            pltpu.VMEM((2, ROWS, DEPTH), bf16),
            pltpu.VMEM((2, DEPTH, WIDE), bf16),
            pltpu.VMEM((DEPTH, WIDE), bf16),
            pltpu.VMEM((4, 4, 2, DEPTH, WIDE), bf16),
            pltpu.VMEM((16, ROWS, WIDE), f32),
            pltpu.VMEM((2, 4, ROWS // 2, WIDE), f32),
            pltpu.VMEM((2, 4, ROWS, WIDE), f32),
            pltpu.VMEM((4, ROWS, WIDE), bf16),
            pltpu.VMEM((2, ROWS, WIDE), bf16),
            dma((3,)),
            dma((2,)),
            dma((2,)),
            dma((4, 4, 2, 4)),
            dma((4, 4, 2)),
            dma((16, 2)),
            dma((6, 4)),
            dma((2,)),
            dma((2,)),
            dma((4,)),
        ],
        compiler_params=pltpu.CompilerParams(
            collective_id=0, has_side_effects=True, vmem_limit_bytes=60 << 20
        ),
    )(amplitudes, integrals, amp_mask, int_mask)


def solution(mesh):
    in_specs = (P("row", "col"), P("col", "row"), P("row", "col"), P("col", "row"))
    out_specs = P("row", "col")
    return jax.shard_map(
        per_device, mesh=mesh, in_specs=in_specs, out_specs=out_specs, check_vma=False
    )
```

```python
import jax
import jax.numpy as jnp
from jax import lax
from jax.experimental import pallas as pl
from jax.experimental.pallas import tpu as pltpu
from jax.sharding import PartitionSpec as P

MESH = pl.DeviceIdType.MESH
TILE = 128
ROWS = 1024
DEPTH = 2048
WIDE = 128
BLOCK = 256
STEP = (0, 3, 1, 2)


def kernel(
    a_hbm, b_hbm, am, im, o_hbm,
    a_buf, b_raw, b_out, b_buf, c_buf, near, mine, out_buf, out_send,
    load_sem, pair_s, pair_r, ring_s, ring_r, y_s, y_r, o_s, o_r, store_sem,
):
    r, q = lax.axis_index("row"), lax.axis_index("col")
    x, z, y, c = r // 4, r % 4, q // 2, q % 2

    def dev(x_, z_, y_, c_):
        return (x_ * 4 + z_, y_ * 2 + c_)

    sibling = dev(x, z, y, 1 - c)
    on_x, on_z = 1 - c, c

    def along_first(d):
        return dev((x + d * on_x) % 4, (z + d * on_z) % 4, y, c)

    def along_second(d):
        return dev((x + d * on_z) % 4, (z + d * on_x) % 4, y, c)

    def along_y(d):
        return dev(x, z, (y + d) % 4, c)

    started = []

    def send(src, dst, ss, rs, to):
        copy = pltpu.make_async_remote_copy(
            src_ref=src, dst_ref=dst, send_sem=ss, recv_sem=rs, device_id=to, device_id_type=MESH
        )
        copy.start()
        return copy

    def arrived(dst, rs):
        pltpu.make_async_remote_copy(
            src_ref=dst, dst_ref=dst, send_sem=rs, recv_sem=rs, device_id=sibling, device_id_type=MESH
        ).wait_recv()

    loads = [
        pltpu.make_async_copy(b_hbm.at[:, pl.ds(h * WIDE, WIDE)], b_raw.at[h], load_sem.at[h])
        for h in range(2)
    ] + [pltpu.make_async_copy(a_hbm, a_buf.at[c], load_sem.at[2])]
    for load in loads:
        load.start()

    barrier = pltpu.get_barrier_semaphore()
    peers = [sibling]
    for d in (1, 3):
        peers += [along_first(d), along_second(d), along_y(d)]
    for peer in peers:
        pl.semaphore_signal(barrier, inc=1, device_id=peer, device_id_type=MESH)

    loads[0].wait()
    loads[1].wait()

    def mask_b(t, carry):
        rows = pl.ds(pl.multiple_of(t * TILE, TILE), TILE)
        keep = im[1 - c, t].astype(jnp.float32)
        b_out[rows, :] = (b_raw[1 - c, rows, :].astype(jnp.float32) * keep).astype(jnp.bfloat16)
        keep = im[c, t].astype(jnp.float32)
        b_buf[0, 0, c, rows, :] = (b_raw[c, rows, :].astype(jnp.float32) * keep).astype(jnp.bfloat16)
        return carry

    lax.fori_loop(0, DEPTH // TILE, mask_b, 0)
    pl.semaphore_wait(barrier, 7)

    def ring(i, j, h, ti, tj, direction, to):
        started.append(
            send(
                b_buf.at[i, j, h], b_buf.at[ti, tj, h],
                ring_s.at[i, j, h, direction], ring_r.at[ti, tj, h], to,
            )
        )

    def got(i, j, h):
        arrived(b_buf.at[i, j, h], ring_r.at[i, j, h])

    def first_out(h):
        ring(0, 0, h, 1, 0, 0, along_first(1))
        ring(0, 0, h, 2, 0, 1, along_first(3))

    started.append(send(b_out, b_buf.at[0, 0, c], pair_s.at[0], pair_r.at[0], sibling))
    first_out(c)

    loads[2].wait()

    def mask_a(t, carry):
        rows = pl.ds(pl.multiple_of(t * TILE, TILE), TILE)
        for k in range(DEPTH // TILE):
            cols = pl.ds(k * TILE, TILE)
            keep = am[t, k].astype(jnp.float32)
            a_buf[c, rows, cols] = (a_buf[c, rows, cols].astype(jnp.float32) * keep).astype(jnp.bfloat16)
        return carry

    lax.fori_loop(0, ROWS // TILE, mask_a, 0)
    arrived(b_buf.at[0, 0, 1 - c], pair_r.at[0])
    first_out(1 - c)
    started.append(send(a_buf.at[c], a_buf.at[c], pair_s.at[1], pair_r.at[1], sibling))

    def first_forward(h):
        got(1 + h, 0, h)
        ring(1 + h, 0, h, 3, 0, h, along_first(1 + 2 * h))

    def second_forward(i, h):
        got(i, 1 + h, h)
        ring(i, 1 + h, h, i, 3, 2 + h, along_second(1 + 2 * h))

    def second_rest(i):
        got(i, 1, 1)
        got(i, 2, 0)

    def second_both(i):
        for h in range(2):
            ring(i, 0, h, i, 1 + h, 2 + h, along_second(1 + 2 * h))
        for h in range(2):
            ring(i, 0, 1 - h, i, 1 + h, 2 + h, along_second(1 + 2 * h))

    def product(*slots):
        def step(t, carry):
            rows = pl.ds(pl.multiple_of(t * BLOCK, BLOCK), BLOCK)
            total = None
            for h in range(2):
                units = [b_buf[i, j, h] for i, j in slots]
                unit = units[0] if len(units) == 1 else jnp.concatenate(units, axis=1)
                part = jnp.dot(a_buf[h, rows, :], unit, preferred_element_type=jnp.float32)
                total = part if total is None else total + part
            for n, (i, j) in enumerate(slots):
                c_buf[i * 4 + j, rows, :] = total[:, n * WIDE : (n + 1) * WIDE]
            return carry

        lax.fori_loop(0, ROWS // BLOCK, step, 0)

    def step_of(i):
        if isinstance(i, int):
            return STEP[i]
        return jnp.where(i == 0, 0, jnp.where(i == 1, 3, i - 1))

    def place(i, j):
        di, dj = step_of(i), step_of(j)
        return (x + di * on_x + dj * on_z) % 4, (z + di * on_z + dj * on_x) % 4

    HALF = ROWS // 2

    def half(n):
        return pl.ds(n * HALF, HALF)

    def y_copy(u, n, dst, ss, rs, to):
        return pltpu.make_async_remote_copy(
            src_ref=c_buf.at[u, half(n)], dst_ref=dst, send_sem=ss, recv_sem=rs, device_id=to, device_id_type=MESH
        )

    def far_copy(u, n, zz):
        return y_copy(u, n, near.at[n, zz], y_s.at[u, n], y_r.at[n, zz], along_y(3 if n == 0 else 1))

    def near_copy(u, n, side, zz):
        return y_copy(
            u, n, mine.at[side, zz, half(n)], y_s.at[u, n], y_r.at[2 + side * 2 + n, zz], along_y(3 if side == 0 else 1)
        )

    def pass_on(i, j):
        u = i * 4 + j
        xx, zz = place(i, j)
        role = (y - xx + 4) % 4

        @pl.when(role == 2)
        def _():
            far_copy(u, 0, zz).start()
            far_copy(u, 1, zz).start()

        @pl.when(role == 1)
        def _():
            near_copy(u, 1, 0, zz).start()

        @pl.when(role == 3)
        def _():
            near_copy(u, 0, 1, zz).start()

    def add_on(i, j):
        u = i * 4 + j
        xx, zz = place(i, j)
        role = (y - xx + 4) % 4

        def add(n, side):
            arrived(near.at[n, zz], y_r.at[n, zz])
            c_buf[u, half(n), :] = c_buf[u, half(n), :] + near[n, zz]
            near_copy(u, n, side, zz).start()

        @pl.when(role == 1)
        def _():
            add(0, 0)

        @pl.when(role == 3)
        def _():
            add(1, 1)

    waiting = []

    def run(*slots, lag=2):
        product(*slots)
        for i, j in slots:
            pass_on(i, j)
        waiting.append(slots)
        settle(lag)

    def settle(lag):
        while len(waiting) > lag:
            for i, j in waiting.pop(0):
                add_on(i, j)

    rel = (y - x + 4) % 4

    def pick(other, *by_rel):
        i = jnp.where(rel == 0, by_rel[0], jnp.where(rel == 1, by_rel[1], jnp.where(rel == 2, by_rel[2], by_rel[3])))
        return jnp.where(c == 1, other, i)

    order = [pick(0, 1, 1, 0, 2), pick(1, 3, 0, 1, 0), pick(2, 2, 3, 2, 3), pick(3, 0, 2, 3, 1)]

    def neighbours(p):
        for h in range(2):
            second_forward(order[p], h)
        second_rest(order[p])
        run((order[p], 1), (order[p], 2))

    def across(p, lag=2):
        for h in range(2):
            got(order[p], 3, h)
        run((order[p], 3), lag=lag)

    arrived(a_buf.at[1 - c], pair_r.at[1])
    run((0, 0))
    for h in (c, 1 - c):
        first_forward(h)
        got(2 - h, 0, h)
    second_both(order[0])
    run((1, 0), (2, 0))
    got(3, 0, 0)
    got(3, 0, 1)
    second_both(order[1])
    run((3, 0))
    neighbours(0)
    second_both(order[2])
    neighbours(1)
    across(0)
    second_both(order[3])
    neighbours(2)
    across(1)
    neighbours(3)
    across(2, lag=1)
    across(3, lag=1)
    settle(0)

    ahead = (y - x + 4) % 4
    slot = (ahead == 1) * 2 + (ahead == 2) * 3 + (ahead == 3) * 1

    def own(j):
        u = jnp.where(c == 0, slot * 4 + j, j * 4 + slot)
        zz = (z + STEP[j]) % 4
        return u, zz

    def store(n):
        return pltpu.make_async_copy(
            out_buf.at[n], o_hbm.at[:, pl.ds(n * WIDE, WIDE)], store_sem.at[n]
        )

    for j in range(4):
        u, zz = own(j)
        for side in range(2):
            for n in range(2):
                arrived(mine.at[side, zz, half(n)], y_r.at[2 + side * 2 + n, zz])
        spot = (zz % 2) * 2 + c
        stays = zz // 2 == c

        def value(t):
            rows = pl.ds(pl.multiple_of(t * TILE, TILE), TILE)
            return rows, (c_buf[u, rows, :] + (mine[0, zz, rows, :] + mine[1, zz, rows, :])).astype(jnp.bfloat16)

        @pl.when(stays)
        def _():
            def step(t, carry):
                rows, v = value(t)
                out_buf[spot, rows, :] = v
                return carry

            lax.fori_loop(0, ROWS // TILE, step, 0)

        @pl.when(jnp.logical_not(stays))
        def _():
            def step(t, carry):
                rows, v = value(t)
                out_send[zz % 2, rows, :] = v
                return carry

            lax.fori_loop(0, ROWS // TILE, step, 0)
            send(out_send.at[zz % 2], out_buf.at[spot], o_s.at[zz % 2], o_r.at[zz % 2], sibling)

    for n in range(2):
        arrived(out_buf.at[n * 2 + 1 - c], o_r.at[n])
    for n in range(4):
        store(n).start()

    for copy in started:
        copy.wait_send()
    for u in range(16):
        i, j = u // 4, u % 4
        xx, zz = place(i, j)
        role = (y - xx + 4) % 4

        @pl.when(role != 0)
        def _():
            for n in range(2):
                far_copy(u, n, zz).wait_send()

    for n in range(2):
        pltpu.make_async_remote_copy(
            src_ref=out_send.at[n], dst_ref=out_send.at[n], send_sem=o_s.at[n], recv_sem=o_s.at[n],
            device_id=sibling, device_id_type=MESH,
        ).wait_send()
    for n in range(4):
        store(n).wait()


def per_device(amplitudes, integrals, amp_mask, int_mask):
    bf16, f32 = jnp.bfloat16, jnp.float32
    dma = pltpu.SemaphoreType.DMA
    return pl.pallas_call(
        kernel,
        out_shape=jax.ShapeDtypeStruct((ROWS, 4 * WIDE), bf16),
        in_specs=[
            pl.BlockSpec(memory_space=pl.ANY),
            pl.BlockSpec(memory_space=pl.ANY),
            pl.BlockSpec(memory_space=pltpu.SMEM),
            pl.BlockSpec(memory_space=pltpu.SMEM),
        ],
        out_specs=pl.BlockSpec(memory_space=pl.ANY),
        scratch_shapes=[
            pltpu.VMEM((2, ROWS, DEPTH), bf16),
            pltpu.VMEM((2, DEPTH, WIDE), bf16),
            pltpu.VMEM((DEPTH, WIDE), bf16),
            pltpu.VMEM((4, 4, 2, DEPTH, WIDE), bf16),
            pltpu.VMEM((16, ROWS, WIDE), f32),
            pltpu.VMEM((2, 4, ROWS // 2, WIDE), f32),
            pltpu.VMEM((2, 4, ROWS, WIDE), f32),
            pltpu.VMEM((4, ROWS, WIDE), bf16),
            pltpu.VMEM((2, ROWS, WIDE), bf16),
            dma((3,)),
            dma((2,)),
            dma((2,)),
            dma((4, 4, 2, 4)),
            dma((4, 4, 2)),
            dma((16, 2)),
            dma((6, 4)),
            dma((2,)),
            dma((2,)),
            dma((4,)),
        ],
        compiler_params=pltpu.CompilerParams(
            collective_id=0, has_side_effects=True, vmem_limit_bytes=60 << 20
        ),
    )(amplitudes, integrals, amp_mask, int_mask.T)


def solution(mesh):
    in_specs = (P("row", "col"), P("col", "row"), P("row", "col"), P("col", "row"))
    out_specs = P("row", "col")
    return jax.shard_map(
        per_device, mesh=mesh, in_specs=in_specs, out_specs=out_specs, check_vma=False
    )
```

```python
import jax
import jax.numpy as jnp
from jax import lax
from jax.experimental import pallas as pl
from jax.experimental.pallas import tpu as pltpu
from jax.sharding import PartitionSpec as P

MESH = pl.DeviceIdType.MESH
TILE = 128
ROWS = 1024
DEPTH = 2048
WIDE = 128
BLOCK = 256
HALF = ROWS // 2
EXTRA = 16
STEPS = 256.0
STEP = (0, 3, 1, 2)


def kernel(
    a_hbm, b_hbm, am, im, o_hbm,
    a_buf, b_raw, b_out, b_buf, c_buf, code, near, mine, out_buf, out_send,
    load_sem, pair_s, pair_r, ring_s, ring_r, y_s, y_r, o_s, o_r, store_sem,
):
    r, q = lax.axis_index("row"), lax.axis_index("col")
    x, z, y, c = r // 4, r % 4, q // 2, q % 2

    def dev(x_, z_, y_, c_):
        return (x_ * 4 + z_, y_ * 2 + c_)

    sibling = dev(x, z, y, 1 - c)
    on_x, on_z = 1 - c, c

    def along_first(d):
        return dev((x + d * on_x) % 4, (z + d * on_z) % 4, y, c)

    def along_second(d):
        return dev((x + d * on_z) % 4, (z + d * on_x) % 4, y, c)

    def along_y(d):
        return dev(x, z, (y + d) % 4, c)

    started = []

    def send(src, dst, ss, rs, to):
        copy = pltpu.make_async_remote_copy(
            src_ref=src, dst_ref=dst, send_sem=ss, recv_sem=rs, device_id=to, device_id_type=MESH
        )
        copy.start()
        return copy

    def arrived(dst, rs):
        pltpu.make_async_remote_copy(
            src_ref=dst, dst_ref=dst, send_sem=rs, recv_sem=rs, device_id=sibling, device_id_type=MESH
        ).wait_recv()

    loads = [
        pltpu.make_async_copy(b_hbm.at[:, pl.ds(h * WIDE, WIDE)], b_raw.at[h], load_sem.at[h])
        for h in range(2)
    ] + [pltpu.make_async_copy(a_hbm, a_buf.at[c], load_sem.at[2])]
    for load in loads:
        load.start()

    barrier = pltpu.get_barrier_semaphore()
    peers = [sibling]
    for d in (1, 3):
        peers += [along_first(d), along_second(d), along_y(d)]
    for peer in peers:
        pl.semaphore_signal(barrier, inc=1, device_id=peer, device_id_type=MESH)

    loads[0].wait()
    loads[1].wait()

    def mask_b(t, carry):
        rows = pl.ds(pl.multiple_of(t * TILE, TILE), TILE)
        keep = im[1 - c, t].astype(jnp.float32)
        b_out[rows, :] = (b_raw[1 - c, rows, :].astype(jnp.float32) * keep).astype(jnp.bfloat16)
        keep = im[c, t].astype(jnp.float32)
        b_buf[0, 0, c, rows, :] = (b_raw[c, rows, :].astype(jnp.float32) * keep).astype(jnp.bfloat16)
        return carry

    lax.fori_loop(0, DEPTH // TILE, mask_b, 0)
    pl.semaphore_wait(barrier, 7)

    def ring(i, j, h, ti, tj, direction, to):
        started.append(
            send(
                b_buf.at[i, j, h], b_buf.at[ti, tj, h],
                ring_s.at[i, j, h, direction], ring_r.at[ti, tj, h], to,
            )
        )

    def got(i, j, h):
        arrived(b_buf.at[i, j, h], ring_r.at[i, j, h])

    def first_out(h):
        ring(0, 0, h, 1, 0, 0, along_first(1))
        ring(0, 0, h, 2, 0, 1, along_first(3))

    started.append(send(b_out, b_buf.at[0, 0, c], pair_s.at[0], pair_r.at[0], sibling))
    first_out(c)

    loads[2].wait()

    def mask_a(t, carry):
        rows = pl.ds(pl.multiple_of(t * TILE, TILE), TILE)
        for k in range(DEPTH // TILE):
            cols = pl.ds(k * TILE, TILE)
            keep = am[t, k].astype(jnp.float32)
            a_buf[c, rows, cols] = (a_buf[c, rows, cols].astype(jnp.float32) * keep).astype(jnp.bfloat16)
        return carry

    lax.fori_loop(0, ROWS // TILE, mask_a, 0)
    arrived(b_buf.at[0, 0, 1 - c], pair_r.at[0])
    first_out(1 - c)
    started.append(send(a_buf.at[c], a_buf.at[c], pair_s.at[1], pair_r.at[1], sibling))

    def first_forward(h):
        got(1 + h, 0, h)
        ring(1 + h, 0, h, 3, 0, h, along_first(1 + 2 * h))

    def second_forward(i, h):
        got(i, 1 + h, h)
        ring(i, 1 + h, h, i, 3, 2 + h, along_second(1 + 2 * h))

    def second_rest(i):
        got(i, 1, 1)
        got(i, 2, 0)

    def second_both(i):
        for h in range(2):
            ring(i, 0, h, i, 1 + h, 2 + h, along_second(1 + 2 * h))
        for h in range(2):
            ring(i, 0, 1 - h, i, 1 + h, 2 + h, along_second(1 + 2 * h))

    def product(*slots):
        def step(t, carry):
            rows = pl.ds(pl.multiple_of(t * BLOCK, BLOCK), BLOCK)
            total = None
            for h in range(2):
                units = [b_buf[i, j, h] for i, j in slots]
                unit = units[0] if len(units) == 1 else jnp.concatenate(units, axis=1)
                part = jnp.dot(a_buf[h, rows, :], unit, preferred_element_type=jnp.float32)
                total = part if total is None else total + part
            for n, (i, j) in enumerate(slots):
                c_buf[i * 4 + j, rows, :] = total[:, n * WIDE : (n + 1) * WIDE]
            return carry

        lax.fori_loop(0, ROWS // BLOCK, step, 0)

    def step_of(i):
        if isinstance(i, int):
            return STEP[i]
        return jnp.where(i == 0, 0, jnp.where(i == 1, 3, i - 1))

    def place(i, j):
        di, dj = step_of(i), step_of(j)
        return (x + di * on_x + dj * on_z) % 4, (z + di * on_z + dj * on_x) % 4

    def half(n):
        return pl.ds(n * HALF, HALF)

    def pack(u, n):
        blocks = [pl.ds(t * TILE, TILE) for t in range(HALF // TILE)]
        top = jnp.full((1, WIDE), 1e-30, jnp.float32)
        for rows in blocks:
            top = jnp.maximum(top, jnp.max(jnp.abs(c_buf.at[u, half(n)][rows, :]), axis=0, keepdims=True))
        level = jnp.floor(STEPS * jnp.log2(32000.0 / top))
        scale = jnp.exp2(level / STEPS)
        for rows in blocks:
            value = jnp.floor(c_buf.at[u, half(n)][rows, :] * scale + 0.5)
            code[u, n, rows, :] = value.astype(jnp.int32).astype(jnp.int16)
        code[u, n, pl.ds(HALF, EXTRA), :] = (
            jnp.broadcast_to(level, (EXTRA, WIDE)).astype(jnp.int32).astype(jnp.int16)
        )

    def size_of(ref):
        level = ref[pl.ds(HALF, EXTRA), :].astype(jnp.int32).astype(jnp.float32)
        return jnp.exp2(-level[:1, :] / STEPS)

    def decode(ref, rows, size):
        return ref[rows, :].astype(jnp.int32).astype(jnp.float32) * size

    def y_copy(u, n, dst, ss, rs, to):
        return pltpu.make_async_remote_copy(
            src_ref=code.at[u, n], dst_ref=dst, send_sem=ss, recv_sem=rs, device_id=to, device_id_type=MESH
        )

    def far_copy(u, n, zz):
        return y_copy(u, n, near.at[n, zz], y_s.at[u, n], y_r.at[n, zz], along_y(3 if n == 0 else 1))

    def near_copy(u, n, side, zz):
        return y_copy(
            u, n, mine.at[side, zz, n], y_s.at[u, n], y_r.at[2 + side * 2 + n, zz], along_y(3 if side == 0 else 1)
        )

    def pass_on(i, j):
        u = i * 4 + j
        xx, zz = place(i, j)
        role = (y - xx + 4) % 4

        @pl.when(role == 2)
        def _():
            for n in range(2):
                pack(u, n)
                far_copy(u, n, zz).start()

        @pl.when(role == 1)
        def _():
            pack(u, 1)
            near_copy(u, 1, 0, zz).start()

        @pl.when(role == 3)
        def _():
            pack(u, 0)
            near_copy(u, 0, 1, zz).start()

    def add_on(i, j):
        u = i * 4 + j
        xx, zz = place(i, j)
        role = (y - xx + 4) % 4

        def add(n, side):
            ref = near.at[n, zz]
            arrived(ref, y_r.at[n, zz])
            size = size_of(ref)
            for t in range(HALF // TILE):
                rows = pl.ds(t * TILE, TILE)
                c_buf.at[u, half(n)][rows, :] = c_buf.at[u, half(n)][rows, :] + decode(ref, rows, size)
            pack(u, n)
            near_copy(u, n, side, zz).start()

        @pl.when(role == 1)
        def _():
            add(0, 0)

        @pl.when(role == 3)
        def _():
            add(1, 1)

    waiting = []

    def run(*slots, lag=2):
        product(*slots)
        for i, j in slots:
            pass_on(i, j)
        waiting.append(slots)
        settle(lag)

    def settle(lag):
        while len(waiting) > lag:
            for i, j in waiting.pop(0):
                add_on(i, j)

    rel = (y - x + 4) % 4

    def pick(other, *by_rel):
        i = jnp.where(rel == 0, by_rel[0], jnp.where(rel == 1, by_rel[1], jnp.where(rel == 2, by_rel[2], by_rel[3])))
        return jnp.where(c == 1, other, i)

    order = [pick(0, 1, 1, 0, 2), pick(1, 3, 0, 1, 0), pick(2, 2, 3, 2, 3), pick(3, 0, 2, 3, 1)]

    def neighbours(p):
        for h in range(2):
            second_forward(order[p], h)
        second_rest(order[p])
        run((order[p], 1), (order[p], 2))

    def across(p, lag=2):
        for h in range(2):
            got(order[p], 3, h)
        run((order[p], 3), lag=lag)

    arrived(a_buf.at[1 - c], pair_r.at[1])
    run((0, 0))
    for h in (c, 1 - c):
        first_forward(h)
        got(2 - h, 0, h)
    second_both(order[0])
    run((1, 0), (2, 0))
    got(3, 0, 0)
    got(3, 0, 1)
    second_both(order[1])
    run((3, 0))
    neighbours(0)
    second_both(order[2])
    neighbours(1)
    across(0)
    second_both(order[3])
    neighbours(2)
    across(1)
    neighbours(3)
    across(2, lag=1)
    across(3, lag=1)
    settle(0)

    ahead = (y - x + 4) % 4
    slot = (ahead == 1) * 2 + (ahead == 2) * 3 + (ahead == 3) * 1

    def own(j):
        u = jnp.where(c == 0, slot * 4 + j, j * 4 + slot)
        zz = (z + STEP[j]) % 4
        return u, zz

    def store(n):
        return pltpu.make_async_copy(
            out_buf.at[n], o_hbm.at[:, pl.ds(n * WIDE, WIDE)], store_sem.at[n]
        )

    for j in range(4):
        u, zz = own(j)
        spot = (zz % 2) * 2 + c
        stays = zz // 2 == c

        def finish(put):
            for n in range(2):
                refs = [mine.at[side, zz, n] for side in range(2)]
                for side in range(2):
                    arrived(refs[side], y_r.at[2 + side * 2 + n, zz])
                sizes = [size_of(ref) for ref in refs]
                for t in range(HALF // TILE):
                    rows = pl.ds(t * TILE, TILE)
                    others = [decode(ref, rows, size) for ref, size in zip(refs, sizes)]
                    value = c_buf.at[u, half(n)][rows, :] + (others[0] + others[1])
                    put(pl.ds(n * HALF + t * TILE, TILE), value.astype(jnp.bfloat16))

        @pl.when(stays)
        def _():
            def put(rows, value):
                out_buf[spot, rows, :] = value

            finish(put)

        @pl.when(jnp.logical_not(stays))
        def _():
            def put(rows, value):
                out_send[zz % 2, rows, :] = value

            finish(put)
            send(out_send.at[zz % 2], out_buf.at[spot], o_s.at[zz % 2], o_r.at[zz % 2], sibling)

    for n in range(2):
        arrived(out_buf.at[n * 2 + 1 - c], o_r.at[n])
    for n in range(4):
        store(n).start()

    for copy in started:
        copy.wait_send()
    for u in range(16):
        i, j = u // 4, u % 4
        xx, zz = place(i, j)
        role = (y - xx + 4) % 4

        @pl.when(role != 0)
        def _():
            for n in range(2):
                far_copy(u, n, zz).wait_send()

    for n in range(2):
        pltpu.make_async_remote_copy(
            src_ref=out_send.at[n], dst_ref=out_send.at[n], send_sem=o_s.at[n], recv_sem=o_s.at[n],
            device_id=sibling, device_id_type=MESH,
        ).wait_send()
    for n in range(4):
        store(n).wait()


def per_device(amplitudes, integrals, amp_mask, int_mask):
    bf16, f32 = jnp.bfloat16, jnp.float32
    dma = pltpu.SemaphoreType.DMA
    return pl.pallas_call(
        kernel,
        out_shape=jax.ShapeDtypeStruct((ROWS, 4 * WIDE), bf16),
        in_specs=[
            pl.BlockSpec(memory_space=pl.ANY),
            pl.BlockSpec(memory_space=pl.ANY),
            pl.BlockSpec(memory_space=pltpu.SMEM),
            pl.BlockSpec(memory_space=pltpu.SMEM),
        ],
        out_specs=pl.BlockSpec(memory_space=pl.ANY),
        scratch_shapes=[
            pltpu.VMEM((2, ROWS, DEPTH), bf16),
            pltpu.VMEM((2, DEPTH, WIDE), bf16),
            pltpu.VMEM((DEPTH, WIDE), bf16),
            pltpu.VMEM((4, 4, 2, DEPTH, WIDE), bf16),
            pltpu.VMEM((16, ROWS, WIDE), f32),
            pltpu.VMEM((16, 2, HALF + EXTRA, WIDE), jnp.int16),
            pltpu.VMEM((2, 4, HALF + EXTRA, WIDE), jnp.int16),
            pltpu.VMEM((2, 4, 2, HALF + EXTRA, WIDE), jnp.int16),
            pltpu.VMEM((4, ROWS, WIDE), bf16),
            pltpu.VMEM((2, ROWS, WIDE), bf16),
            dma((3,)),
            dma((2,)),
            dma((2,)),
            dma((4, 4, 2, 4)),
            dma((4, 4, 2)),
            dma((16, 2)),
            dma((6, 4)),
            dma((2,)),
            dma((2,)),
            dma((4,)),
        ],
        compiler_params=pltpu.CompilerParams(
            collective_id=0, has_side_effects=True, vmem_limit_bytes=60 << 20
        ),
    )(amplitudes, integrals, amp_mask, int_mask.T)


def solution(mesh):
    in_specs = (P("row", "col"), P("col", "row"), P("row", "col"), P("col", "row"))
    out_specs = P("row", "col")
    return jax.shard_map(
        per_device, mesh=mesh, in_specs=in_specs, out_specs=out_specs, check_vma=False
    )
```

```python
import jax
import jax.numpy as jnp
from jax import lax
from jax.experimental import pallas as pl
from jax.experimental.pallas import tpu as pltpu
from jax.sharding import PartitionSpec as P

MESH = pl.DeviceIdType.MESH
TILE = 128
ROWS = 1024
DEPTH = 2048
WIDE = 128
BLOCK = 256
HALF = ROWS // 2
EXTRA = 16
STEPS = 256.0
STEP = (0, 3, 1, 2)


def kernel(
    a_hbm, b_hbm, am, im, o_ref,
    a_buf, b_raw, b_out, b_buf, c_buf, code, near, mine, out_send,
    load_sem, pair_s, pair_r, ring_s, ring_r, y_s, y_r, o_s, o_r,
):
    r, q = lax.axis_index("row"), lax.axis_index("col")
    x, z, y, c = r // 4, r % 4, q // 2, q % 2

    def dev(x_, z_, y_, c_):
        return (x_ * 4 + z_, y_ * 2 + c_)

    sibling = dev(x, z, y, 1 - c)
    on_x, on_z = 1 - c, c

    def along_first(d):
        return dev((x + d * on_x) % 4, (z + d * on_z) % 4, y, c)

    def along_second(d):
        return dev((x + d * on_z) % 4, (z + d * on_x) % 4, y, c)

    def along_y(d):
        return dev(x, z, (y + d) % 4, c)

    started = []

    def send(src, dst, ss, rs, to):
        copy = pltpu.make_async_remote_copy(
            src_ref=src, dst_ref=dst, send_sem=ss, recv_sem=rs, device_id=to, device_id_type=MESH
        )
        copy.start()
        return copy

    def arrived(dst, rs):
        pltpu.make_async_remote_copy(
            src_ref=dst, dst_ref=dst, send_sem=rs, recv_sem=rs, device_id=sibling, device_id_type=MESH
        ).wait_recv()

    loads = [
        pltpu.make_async_copy(b_hbm.at[:, pl.ds(h * WIDE, WIDE)], b_raw.at[h], load_sem.at[h])
        for h in range(2)
    ] + [pltpu.make_async_copy(a_hbm, a_buf.at[c], load_sem.at[2])]
    for load in loads:
        load.start()

    barrier = pltpu.get_barrier_semaphore()
    peers = [sibling]
    for d in (1, 3):
        peers += [along_first(d), along_second(d), along_y(d)]
    for peer in peers:
        pl.semaphore_signal(barrier, inc=1, device_id=peer, device_id_type=MESH)

    loads[0].wait()
    loads[1].wait()

    def mask_b(t, carry):
        rows = pl.ds(pl.multiple_of(t * TILE, TILE), TILE)
        keep = im[1 - c, t].astype(jnp.float32)
        b_out[rows, :] = (b_raw[1 - c, rows, :].astype(jnp.float32) * keep).astype(jnp.bfloat16)
        keep = im[c, t].astype(jnp.float32)
        b_buf[0, 0, c, rows, :] = (b_raw[c, rows, :].astype(jnp.float32) * keep).astype(jnp.bfloat16)
        return carry

    lax.fori_loop(0, DEPTH // TILE, mask_b, 0)
    pl.semaphore_wait(barrier, 7)

    def ring(i, j, h, ti, tj, direction, to):
        started.append(
            send(
                b_buf.at[i, j, h], b_buf.at[ti, tj, h],
                ring_s.at[i, j, h, direction], ring_r.at[ti, tj, h], to,
            )
        )

    def got(i, j, h):
        arrived(b_buf.at[i, j, h], ring_r.at[i, j, h])

    def first_out(h):
        ring(0, 0, h, 1, 0, 0, along_first(1))
        ring(0, 0, h, 2, 0, 1, along_first(3))

    started.append(send(b_out, b_buf.at[0, 0, c], pair_s.at[0], pair_r.at[0], sibling))
    first_out(c)

    loads[2].wait()

    def mask_a(t, carry):
        rows = pl.ds(pl.multiple_of(t * TILE, TILE), TILE)
        for k in range(DEPTH // TILE):
            cols = pl.ds(k * TILE, TILE)
            keep = am[t, k].astype(jnp.float32)
            a_buf[c, rows, cols] = (a_buf[c, rows, cols].astype(jnp.float32) * keep).astype(jnp.bfloat16)
        return carry

    lax.fori_loop(0, ROWS // TILE, mask_a, 0)
    arrived(b_buf.at[0, 0, 1 - c], pair_r.at[0])
    first_out(1 - c)
    started.append(send(a_buf.at[c], a_buf.at[c], pair_s.at[1], pair_r.at[1], sibling))

    def first_forward(h):
        got(1 + h, 0, h)
        ring(1 + h, 0, h, 3, 0, h, along_first(1 + 2 * h))

    def second_forward(i, h):
        got(i, 1 + h, h)
        ring(i, 1 + h, h, i, 3, 2 + h, along_second(1 + 2 * h))

    def second_rest(i):
        got(i, 1, 1)
        got(i, 2, 0)

    def second_both(i):
        for h in range(2):
            ring(i, 0, h, i, 1 + h, 2 + h, along_second(1 + 2 * h))
        for h in range(2):
            ring(i, 0, 1 - h, i, 1 + h, 2 + h, along_second(1 + 2 * h))

    def product(*slots, first=0, last=ROWS // BLOCK):
        def step(t, carry):
            rows = pl.ds(pl.multiple_of(t * BLOCK, BLOCK), BLOCK)
            total = None
            for h in range(2):
                units = [b_buf[i, j, h] for i, j in slots]
                unit = units[0] if len(units) == 1 else jnp.concatenate(units, axis=1)
                part = jnp.dot(a_buf[h, rows, :], unit, preferred_element_type=jnp.float32)
                total = part if total is None else total + part
            for n, (i, j) in enumerate(slots):
                c_buf[i * 4 + j, rows, :] = total[:, n * WIDE : (n + 1) * WIDE]
            return carry

        lax.fori_loop(first, last, step, 0)

    def step_of(i):
        if isinstance(i, int):
            return STEP[i]
        return jnp.where(i == 0, 0, jnp.where(i == 1, 3, i - 1))

    def place(i, j):
        di, dj = step_of(i), step_of(j)
        return (x + di * on_x + dj * on_z) % 4, (z + di * on_z + dj * on_x) % 4

    def half(n):
        return pl.ds(n * HALF, HALF)

    def pack(u, n):
        blocks = [pl.ds(t * TILE, TILE) for t in range(HALF // TILE)]
        top = jnp.full((1, WIDE), 1e-30, jnp.float32)
        for rows in blocks:
            top = jnp.maximum(top, jnp.max(jnp.abs(c_buf.at[u, half(n)][rows, :]), axis=0, keepdims=True))
        level = jnp.floor(STEPS * jnp.log2(32000.0 / top))
        scale = jnp.exp2(level / STEPS)
        for rows in blocks:
            value = jnp.floor(c_buf.at[u, half(n)][rows, :] * scale + 0.5)
            code[u, n, rows, :] = value.astype(jnp.int32).astype(jnp.int16)
        code[u, n, pl.ds(HALF, EXTRA), :] = (
            jnp.broadcast_to(level, (EXTRA, WIDE)).astype(jnp.int32).astype(jnp.int16)
        )

    def size_of(ref):
        level = ref[pl.ds(HALF, EXTRA), :].astype(jnp.int32).astype(jnp.float32)
        return jnp.exp2(-level[:1, :] / STEPS)

    def decode(ref, rows, size):
        return ref[rows, :].astype(jnp.int32).astype(jnp.float32) * size

    def y_copy(u, n, dst, ss, rs, to):
        return pltpu.make_async_remote_copy(
            src_ref=code.at[u, n], dst_ref=dst, send_sem=ss, recv_sem=rs, device_id=to, device_id_type=MESH
        )

    def far_copy(u, n, zz):
        return y_copy(u, n, near.at[n, zz], y_s.at[u, n], y_r.at[n, zz], along_y(3 if n == 0 else 1))

    def near_copy(u, n, side, zz):
        return y_copy(
            u, n, mine.at[side, zz, n], y_s.at[u, n], y_r.at[2 + side * 2 + n, zz], along_y(3 if side == 0 else 1)
        )

    def pass_on(i, j, n):
        u = i * 4 + j
        xx, zz = place(i, j)
        role = (y - xx + 4) % 4

        @pl.when(role == 2)
        def _():
            pack(u, n)
            far_copy(u, n, zz).start()

        @pl.when(role == (1 if n == 1 else 3))
        def _():
            pack(u, n)
            near_copy(u, n, 1 - n, zz).start()

    def add_on(i, j):
        u = i * 4 + j
        xx, zz = place(i, j)
        role = (y - xx + 4) % 4

        def add(n, side):
            ref = near.at[n, zz]
            arrived(ref, y_r.at[n, zz])
            size = size_of(ref)
            for t in range(HALF // TILE):
                rows = pl.ds(t * TILE, TILE)
                c_buf.at[u, half(n)][rows, :] = c_buf.at[u, half(n)][rows, :] + decode(ref, rows, size)
            pack(u, n)
            near_copy(u, n, side, zz).start()

        @pl.when(role == 1)
        def _():
            add(0, 0)

        @pl.when(role == 3)
        def _():
            add(1, 1)

    waiting = []

    def run(*slots, lag=2):
        product(*slots)
        for i, j in slots:
            for n in range(2):
                pass_on(i, j, n)
        waiting.append(slots)
        settle(lag)

    def settle(lag):
        while len(waiting) > lag:
            for i, j in waiting.pop(0):
                add_on(i, j)

    rel = (y - x + 4) % 4

    def pick(other, *by_rel):
        i = jnp.where(rel == 0, by_rel[0], jnp.where(rel == 1, by_rel[1], jnp.where(rel == 2, by_rel[2], by_rel[3])))
        return jnp.where(c == 1, other, i)

    order = [pick(0, 1, 1, 0, 2), pick(1, 3, 0, 1, 0), pick(2, 2, 3, 2, 3), pick(3, 0, 2, 3, 1)]

    def neighbours(p):
        for h in range(2):
            second_forward(order[p], h)
        second_rest(order[p])
        run((order[p], 1), (order[p], 2))

    def across(p, lag=2):
        for h in range(2):
            got(order[p], 3, h)
        run((order[p], 3), lag=lag)

    ahead = (y - x + 4) % 4
    slot = (ahead == 1) * 2 + (ahead == 2) * 3 + (ahead == 3) * 1

    def out_at(spot):
        return o_ref.at[:, pl.ds(pl.multiple_of(spot * WIDE, WIDE), WIDE)]

    def finish(p):
        u = jnp.where(c == 0, slot * 4 + p, p * 4 + slot)
        zz = (z + STEP[p]) % 4
        spot = (zz % 2) * 2 + c
        stays = zz // 2 == c

        def total(ref):
            for n in range(2):
                refs = [mine.at[side, zz, n] for side in range(2)]
                for side in range(2):
                    arrived(refs[side], y_r.at[2 + side * 2 + n, zz])
                sizes = [size_of(r) for r in refs]
                for t in range(HALF // TILE):
                    rows = pl.ds(t * TILE, TILE)
                    others = [decode(r, rows, size) for r, size in zip(refs, sizes)]
                    value = c_buf.at[u, half(n)][rows, :] + (others[0] + others[1])
                    ref[pl.ds(n * HALF + t * TILE, TILE), :] = value.astype(jnp.bfloat16)

        @pl.when(stays)
        def _():
            total(out_at(spot))

        @pl.when(jnp.logical_not(stays))
        def _():
            total(out_send.at[zz % 2])
            send(out_send.at[zz % 2], out_at(spot), o_s.at[zz % 2], o_r.at[zz % 2], sibling)

    arrived(a_buf.at[1 - c], pair_r.at[1])
    run((0, 0))
    for h in (c, 1 - c):
        first_forward(h)
        got(2 - h, 0, h)
    second_both(order[0])
    run((1, 0), (2, 0))
    got(3, 0, 0)
    got(3, 0, 1)
    second_both(order[1])
    run((3, 0))
    neighbours(0)
    second_both(order[2])
    neighbours(1)
    across(0)
    second_both(order[3])
    neighbours(2)
    across(1)
    neighbours(3)
    across(2, lag=0)
    for j in range(3):
        finish(j)
    for h in range(2):
        got(order[3], 3, h)
    for n in range(2):
        product((order[3], 3), first=2 * n, last=2 * n + 2)
        pass_on(order[3], 3, n)
    add_on(order[3], 3)
    finish(3)
    for n in range(2):
        arrived(out_at(n * 2 + 1 - c), o_r.at[n])

    for copy in started:
        copy.wait_send()
    for u in range(16):
        i, j = u // 4, u % 4
        xx, zz = place(i, j)
        role = (y - xx + 4) % 4

        @pl.when(role != 0)
        def _():
            for n in range(2):
                far_copy(u, n, zz).wait_send()

    for n in range(2):
        pltpu.make_async_remote_copy(
            src_ref=out_send.at[n], dst_ref=out_send.at[n], send_sem=o_s.at[n], recv_sem=o_s.at[n],
            device_id=sibling, device_id_type=MESH,
        ).wait_send()


def per_device(amplitudes, integrals, amp_mask, int_mask):
    bf16, f32 = jnp.bfloat16, jnp.float32
    dma = pltpu.SemaphoreType.DMA
    return pl.pallas_call(
        kernel,
        out_shape=jax.ShapeDtypeStruct((ROWS, 4 * WIDE), bf16),
        in_specs=[
            pl.BlockSpec(memory_space=pl.ANY),
            pl.BlockSpec(memory_space=pl.ANY),
            pl.BlockSpec(memory_space=pltpu.SMEM),
            pl.BlockSpec(memory_space=pltpu.SMEM),
        ],
        out_specs=pl.BlockSpec(memory_space=pltpu.VMEM),
        scratch_shapes=[
            pltpu.VMEM((2, ROWS, DEPTH), bf16),
            pltpu.VMEM((2, DEPTH, WIDE), bf16),
            pltpu.VMEM((DEPTH, WIDE), bf16),
            pltpu.VMEM((4, 4, 2, DEPTH, WIDE), bf16),
            pltpu.VMEM((16, ROWS, WIDE), f32),
            pltpu.VMEM((16, 2, HALF + EXTRA, WIDE), jnp.int16),
            pltpu.VMEM((2, 4, HALF + EXTRA, WIDE), jnp.int16),
            pltpu.VMEM((2, 4, 2, HALF + EXTRA, WIDE), jnp.int16),
            pltpu.VMEM((2, ROWS, WIDE), bf16),
            dma((3,)),
            dma((2,)),
            dma((2,)),
            dma((4, 4, 2, 4)),
            dma((4, 4, 2)),
            dma((16, 2)),
            dma((6, 4)),
            dma((2,)),
            dma((2,)),
        ],
        compiler_params=pltpu.CompilerParams(
            collective_id=0, has_side_effects=True, vmem_limit_bytes=52 << 20
        ),
    )(amplitudes, integrals, amp_mask, int_mask.T)


def solution(mesh):
    in_specs = (P("row", "col"), P("col", "row"), P("row", "col"), P("col", "row"))
    out_specs = P("row", "col")
    return jax.shard_map(
        per_device, mesh=mesh, in_specs=in_specs, out_specs=out_specs, check_vma=False
    )
```

```python
import jax
import jax.numpy as jnp
from jax import lax
from jax.experimental import pallas as pl
from jax.experimental.pallas import tpu as pltpu
from jax.sharding import PartitionSpec as P

MESH = pl.DeviceIdType.MESH
TILE = 128
ROWS = 1024
DEPTH = 2048
WIDE = 128
BLOCK = 256
HALF = ROWS // 2
EXTRA = 16
STEPS = 256.0
STEP = (0, 3, 1, 2)


def kernel(
    a_hbm, b_hbm, am, im, o_ref,
    a_buf, b_raw, b_out, b_buf, c_buf, code, near, mine, out_send,
    load_sem, pair_s, pair_r, ring_s, ring_r, y_s, y_r, o_s, o_r,
):
    r, q = lax.axis_index("row"), lax.axis_index("col")
    x, z, y, c = r // 4, r % 4, q // 2, q % 2

    def dev(x_, z_, y_, c_):
        return (x_ * 4 + z_, y_ * 2 + c_)

    sibling = dev(x, z, y, 1 - c)
    on_x, on_z = 1 - c, c

    def along_first(d):
        return dev((x + d * on_x) % 4, (z + d * on_z) % 4, y, c)

    def along_second(d):
        return dev((x + d * on_z) % 4, (z + d * on_x) % 4, y, c)

    def along_y(d):
        return dev(x, z, (y + d) % 4, c)

    started = []

    def send(src, dst, ss, rs, to):
        copy = pltpu.make_async_remote_copy(
            src_ref=src, dst_ref=dst, send_sem=ss, recv_sem=rs, device_id=to, device_id_type=MESH
        )
        copy.start()
        return copy

    def arrived(dst, rs):
        pltpu.make_async_remote_copy(
            src_ref=dst, dst_ref=dst, send_sem=rs, recv_sem=rs, device_id=sibling, device_id_type=MESH
        ).wait_recv()

    loads = [
        pltpu.make_async_copy(b_hbm.at[:, pl.ds(h * WIDE, WIDE)], b_raw.at[h], load_sem.at[h])
        for h in range(2)
    ] + [pltpu.make_async_copy(a_hbm, a_buf.at[c], load_sem.at[2])]
    for load in loads:
        load.start()

    barrier = pltpu.get_barrier_semaphore()
    peers = [sibling]
    for d in (1, 3):
        peers += [along_first(d), along_second(d), along_y(d)]
    for peer in peers:
        pl.semaphore_signal(barrier, inc=1, device_id=peer, device_id_type=MESH)

    loads[0].wait()
    loads[1].wait()

    def mask_b(t, carry):
        rows = pl.ds(pl.multiple_of(t * TILE, TILE), TILE)
        keep = im[1 - c, t].astype(jnp.float32)
        b_out[rows, :] = (b_raw[1 - c, rows, :].astype(jnp.float32) * keep).astype(jnp.bfloat16)
        keep = im[c, t].astype(jnp.float32)
        b_buf[0, 0, c, rows, :] = (b_raw[c, rows, :].astype(jnp.float32) * keep).astype(jnp.bfloat16)
        return carry

    lax.fori_loop(0, DEPTH // TILE, mask_b, 0)
    pl.semaphore_wait(barrier, 7)

    def ring(i, j, h, ti, tj, direction, to):
        started.append(
            send(
                b_buf.at[i, j, h], b_buf.at[ti, tj, h],
                ring_s.at[i, j, h, direction], ring_r.at[ti, tj, h], to,
            )
        )

    def got(i, j, h):
        arrived(b_buf.at[i, j, h], ring_r.at[i, j, h])

    def first_out(h):
        ring(0, 0, h, 1, 0, 0, along_first(1))
        ring(0, 0, h, 2, 0, 1, along_first(3))

    started.append(send(b_out, b_buf.at[0, 0, c], pair_s.at[0], pair_r.at[0], sibling))
    first_out(c)

    loads[2].wait()

    def mask_a(t, carry):
        rows = pl.ds(pl.multiple_of(t * TILE, TILE), TILE)
        for k in range(DEPTH // TILE):
            cols = pl.ds(k * TILE, TILE)
            keep = am[t, k].astype(jnp.float32)
            a_buf[c, rows, cols] = (a_buf[c, rows, cols].astype(jnp.float32) * keep).astype(jnp.bfloat16)
        return carry

    lax.fori_loop(0, ROWS // TILE, mask_a, 0)
    arrived(b_buf.at[0, 0, 1 - c], pair_r.at[0])
    first_out(1 - c)
    started.append(send(a_buf.at[c], a_buf.at[c], pair_s.at[1], pair_r.at[1], sibling))

    def first_forward(h):
        got(1 + h, 0, h)
        ring(1 + h, 0, h, 3, 0, h, along_first(1 + 2 * h))

    def second_forward(i, h):
        got(i, 1 + h, h)
        ring(i, 1 + h, h, i, 3, 2 + h, along_second(1 + 2 * h))

    def second_rest(i):
        got(i, 1, 1)
        got(i, 2, 0)

    def second_out(i, h):
        ring(i, 0, h, i, 1, 2, along_second(1))
        ring(i, 0, h, i, 2, 3, along_second(3))

    def second_both(i):
        for h in range(2):
            ring(i, 0, h, i, 1 + h, 2 + h, along_second(1 + 2 * h))
        for h in range(2):
            ring(i, 0, 1 - h, i, 1 + h, 2 + h, along_second(1 + 2 * h))

    def product(*slots, first=0, last=ROWS // BLOCK):
        def step(t, carry):
            rows = pl.ds(pl.multiple_of(t * BLOCK, BLOCK), BLOCK)
            total = None
            for h in range(2):
                units = [b_buf[i, j, h] for i, j in slots]
                unit = units[0] if len(units) == 1 else jnp.concatenate(units, axis=1)
                part = jnp.dot(a_buf[h, rows, :], unit, preferred_element_type=jnp.float32)
                total = part if total is None else total + part
            for n, (i, j) in enumerate(slots):
                c_buf[i * 4 + j, rows, :] = total[:, n * WIDE : (n + 1) * WIDE]
            return carry

        lax.fori_loop(first, last, step, 0)

    def step_of(i):
        if isinstance(i, int):
            return STEP[i]
        return jnp.where(i == 0, 0, jnp.where(i == 1, 3, i - 1))

    def place(i, j):
        di, dj = step_of(i), step_of(j)
        return (x + di * on_x + dj * on_z) % 4, (z + di * on_z + dj * on_x) % 4

    def half(n):
        return pl.ds(n * HALF, HALF)

    def pack(u, n):
        blocks = [pl.ds(t * TILE, TILE) for t in range(HALF // TILE)]
        top = jnp.full((1, WIDE), 1e-30, jnp.float32)
        for rows in blocks:
            top = jnp.maximum(top, jnp.max(jnp.abs(c_buf.at[u, half(n)][rows, :]), axis=0, keepdims=True))
        level = jnp.floor(STEPS * jnp.log2(32000.0 / top))
        scale = jnp.exp2(level / STEPS)
        for rows in blocks:
            value = jnp.floor(c_buf.at[u, half(n)][rows, :] * scale + 0.5)
            code[u, n, rows, :] = value.astype(jnp.int32).astype(jnp.int16)
        code[u, n, pl.ds(HALF, EXTRA), :] = (
            jnp.broadcast_to(level, (EXTRA, WIDE)).astype(jnp.int32).astype(jnp.int16)
        )

    def size_of(ref):
        level = ref[pl.ds(HALF, EXTRA), :].astype(jnp.int32).astype(jnp.float32)
        return jnp.exp2(-level[:1, :] / STEPS)

    def decode(ref, rows, size):
        return ref[rows, :].astype(jnp.int32).astype(jnp.float32) * size

    def y_copy(u, n, dst, ss, rs, to):
        return pltpu.make_async_remote_copy(
            src_ref=code.at[u, n], dst_ref=dst, send_sem=ss, recv_sem=rs, device_id=to, device_id_type=MESH
        )

    def far_copy(u, n, zz):
        return y_copy(u, n, near.at[n, zz], y_s.at[u, n], y_r.at[n, zz], along_y(3 if n == 0 else 1))

    def near_copy(u, n, side, zz):
        return y_copy(
            u, n, mine.at[side, zz, n], y_s.at[u, n], y_r.at[2 + side * 2 + n, zz], along_y(3 if side == 0 else 1)
        )

    def pass_on(i, j, n):
        u = i * 4 + j
        xx, zz = place(i, j)
        role = (y - xx + 4) % 4

        @pl.when(role == 2)
        def _():
            pack(u, n)
            far_copy(u, n, zz).start()

        @pl.when(role == (1 if n == 1 else 3))
        def _():
            pack(u, n)
            near_copy(u, n, 1 - n, zz).start()

    def add_on(i, j):
        u = i * 4 + j
        xx, zz = place(i, j)
        role = (y - xx + 4) % 4

        def add(n, side):
            ref = near.at[n, zz]
            arrived(ref, y_r.at[n, zz])
            size = size_of(ref)
            for t in range(HALF // TILE):
                rows = pl.ds(t * TILE, TILE)
                c_buf.at[u, half(n)][rows, :] = c_buf.at[u, half(n)][rows, :] + decode(ref, rows, size)
            pack(u, n)
            near_copy(u, n, side, zz).start()

        @pl.when(role == 1)
        def _():
            add(0, 0)

        @pl.when(role == 3)
        def _():
            add(1, 1)

    waiting = []

    def run(*slots, lag=2):
        product(*slots)
        for i, j in slots:
            for n in range(2):
                pass_on(i, j, n)
        waiting.append(slots)
        settle(lag)

    def settle(lag):
        while len(waiting) > lag:
            for i, j in waiting.pop(0):
                add_on(i, j)

    rel = (y - x + 4) % 4

    def pick(other, *by_rel):
        i = jnp.where(rel == 0, by_rel[0], jnp.where(rel == 1, by_rel[1], jnp.where(rel == 2, by_rel[2], by_rel[3])))
        return jnp.where(c == 1, other, i)

    order = [pick(0, 1, 1, 0, 2), pick(1, 3, 0, 1, 0), pick(2, 2, 3, 2, 3), pick(3, 0, 2, 3, 1)]

    def neighbours(p):
        for h in range(2):
            second_forward(order[p], h)
        second_rest(order[p])
        run((order[p], 1), (order[p], 2))

    def across(p, lag=2):
        for h in range(2):
            got(order[p], 3, h)
        run((order[p], 3), lag=lag)

    ahead = (y - x + 4) % 4
    slot = (ahead == 1) * 2 + (ahead == 2) * 3 + (ahead == 3) * 1

    def out_at(spot):
        return o_ref.at[:, pl.ds(pl.multiple_of(spot * WIDE, WIDE), WIDE)]

    def finish(p):
        u = jnp.where(c == 0, slot * 4 + p, p * 4 + slot)
        zz = (z + STEP[p]) % 4
        spot = (zz % 2) * 2 + c
        stays = zz // 2 == c

        def total(ref):
            for n in range(2):
                refs = [mine.at[side, zz, n] for side in range(2)]
                for side in range(2):
                    arrived(refs[side], y_r.at[2 + side * 2 + n, zz])
                sizes = [size_of(r) for r in refs]
                for t in range(HALF // TILE):
                    rows = pl.ds(t * TILE, TILE)
                    others = [decode(r, rows, size) for r, size in zip(refs, sizes)]
                    value = c_buf.at[u, half(n)][rows, :] + (others[0] + others[1])
                    ref[pl.ds(n * HALF + t * TILE, TILE), :] = value.astype(jnp.bfloat16)

        @pl.when(stays)
        def _():
            total(out_at(spot))

        @pl.when(jnp.logical_not(stays))
        def _():
            total(out_send.at[zz % 2])
            send(out_send.at[zz % 2], out_at(spot), o_s.at[zz % 2], o_r.at[zz % 2], sibling)

    arrived(a_buf.at[1 - c], pair_r.at[1])
    run((0, 0))
    for h in (c, 1 - c):
        first_forward(h)
        got(2 - h, 0, h)
        second_out(order[0], h)
    run((1, 0), (2, 0))
    got(3, 0, 0)
    got(3, 0, 1)
    second_both(order[1])
    run((3, 0))
    neighbours(0)
    second_both(order[2])
    neighbours(1)
    across(0)
    second_both(order[3])
    neighbours(2)
    across(1)
    neighbours(3)
    across(2, lag=0)
    for j in range(3):
        finish(j)
    for h in range(2):
        got(order[3], 3, h)
    for n in range(2):
        product((order[3], 3), first=2 * n, last=2 * n + 2)
        pass_on(order[3], 3, n)
    add_on(order[3], 3)
    finish(3)
    for n in range(2):
        arrived(out_at(n * 2 + 1 - c), o_r.at[n])

    for copy in started:
        copy.wait_send()
    for u in range(16):
        i, j = u // 4, u % 4
        xx, zz = place(i, j)
        role = (y - xx + 4) % 4

        @pl.when(role != 0)
        def _():
            for n in range(2):
                far_copy(u, n, zz).wait_send()

    for n in range(2):
        pltpu.make_async_remote_copy(
            src_ref=out_send.at[n], dst_ref=out_send.at[n], send_sem=o_s.at[n], recv_sem=o_s.at[n],
            device_id=sibling, device_id_type=MESH,
        ).wait_send()


def per_device(amplitudes, integrals, amp_mask, int_mask):
    bf16, f32 = jnp.bfloat16, jnp.float32
    dma = pltpu.SemaphoreType.DMA
    return pl.pallas_call(
        kernel,
        out_shape=jax.ShapeDtypeStruct((ROWS, 4 * WIDE), bf16),
        in_specs=[
            pl.BlockSpec(memory_space=pl.ANY),
            pl.BlockSpec(memory_space=pl.ANY),
            pl.BlockSpec(memory_space=pltpu.SMEM),
            pl.BlockSpec(memory_space=pltpu.SMEM),
        ],
        out_specs=pl.BlockSpec(memory_space=pltpu.VMEM),
        scratch_shapes=[
            pltpu.VMEM((2, ROWS, DEPTH), bf16),
            pltpu.VMEM((2, DEPTH, WIDE), bf16),
            pltpu.VMEM((DEPTH, WIDE), bf16),
            pltpu.VMEM((4, 4, 2, DEPTH, WIDE), bf16),
            pltpu.VMEM((16, ROWS, WIDE), f32),
            pltpu.VMEM((16, 2, HALF + EXTRA, WIDE), jnp.int16),
            pltpu.VMEM((2, 4, HALF + EXTRA, WIDE), jnp.int16),
            pltpu.VMEM((2, 4, 2, HALF + EXTRA, WIDE), jnp.int16),
            pltpu.VMEM((2, ROWS, WIDE), bf16),
            dma((3,)),
            dma((2,)),
            dma((2,)),
            dma((4, 4, 2, 4)),
            dma((4, 4, 2)),
            dma((16, 2)),
            dma((6, 4)),
            dma((2,)),
            dma((2,)),
        ],
        compiler_params=pltpu.CompilerParams(
            collective_id=0, has_side_effects=True, vmem_limit_bytes=52 << 20
        ),
    )(amplitudes, integrals, amp_mask, int_mask.T)


def solution(mesh):
    in_specs = (P("row", "col"), P("col", "row"), P("row", "col"), P("col", "row"))
    out_specs = P("row", "col")
    return jax.shard_map(
        per_device, mesh=mesh, in_specs=in_specs, out_specs=out_specs, check_vma=False
    )
```

```python
import jax
import jax.numpy as jnp
from jax import lax
from jax.experimental import pallas as pl
from jax.experimental.pallas import tpu as pltpu
from jax.sharding import PartitionSpec as P

MESH = pl.DeviceIdType.MESH
TILE = 128
ROWS = 1024
DEPTH = 2048
WIDE = 128
BLOCK = 256
HALF = ROWS // 2
EXTRA = 16
STEPS = 256.0
STEP = (0, 3, 1, 2)


def kernel(
    a_hbm, b_hbm, am_hbm, im_hbm, o_ref,
    a_buf, b_raw, b_out, b_buf, c_buf, code, near, mine, out_send, am, im,
    load_sem, pair_s, pair_r, ring_s, ring_r, y_s, y_r, o_s, o_r,
):
    r, q = lax.axis_index("row"), lax.axis_index("col")
    x, z, y, c = r // 4, r % 4, q // 2, q % 2

    def dev(x_, z_, y_, c_):
        return (x_ * 4 + z_, y_ * 2 + c_)

    sibling = dev(x, z, y, 1 - c)
    on_x, on_z = 1 - c, c

    def along_first(d):
        return dev((x + d * on_x) % 4, (z + d * on_z) % 4, y, c)

    def along_second(d):
        return dev((x + d * on_z) % 4, (z + d * on_x) % 4, y, c)

    def along_y(d):
        return dev(x, z, (y + d) % 4, c)

    started = []

    def send(src, dst, ss, rs, to):
        copy = pltpu.make_async_remote_copy(
            src_ref=src, dst_ref=dst, send_sem=ss, recv_sem=rs, device_id=to, device_id_type=MESH
        )
        copy.start()
        return copy

    def arrived(dst, rs):
        pltpu.make_async_remote_copy(
            src_ref=dst, dst_ref=dst, send_sem=rs, recv_sem=rs, device_id=sibling, device_id_type=MESH
        ).wait_recv()

    loads = [
        pltpu.make_async_copy(b_hbm.at[:, pl.ds(h * WIDE, WIDE)], b_raw.at[h], load_sem.at[h])
        for h in range(2)
    ] + [pltpu.make_async_copy(a_hbm, a_buf.at[c], load_sem.at[2])]
    masks = [
        pltpu.make_async_copy(im_hbm, im, load_sem.at[3]),
        pltpu.make_async_copy(am_hbm, am, load_sem.at[4]),
    ]
    for mask in masks:
        mask.start()
    for load in loads:
        load.start()

    barrier = pltpu.get_barrier_semaphore()
    peers = [sibling]
    for d in (1, 3):
        peers += [along_first(d), along_second(d), along_y(d)]
    for peer in peers:
        pl.semaphore_signal(barrier, inc=1, device_id=peer, device_id_type=MESH)

    loads[0].wait()
    loads[1].wait()
    masks[0].wait()

    def mask_b(t, carry):
        rows = pl.ds(pl.multiple_of(t * TILE, TILE), TILE)
        keep = im[1 - c, t].astype(jnp.float32)
        b_out[rows, :] = (b_raw[1 - c, rows, :].astype(jnp.float32) * keep).astype(jnp.bfloat16)
        keep = im[c, t].astype(jnp.float32)
        b_buf[0, 0, c, rows, :] = (b_raw[c, rows, :].astype(jnp.float32) * keep).astype(jnp.bfloat16)
        return carry

    lax.fori_loop(0, DEPTH // TILE, mask_b, 0)
    pl.semaphore_wait(barrier, 7)

    def ring(i, j, h, ti, tj, direction, to):
        started.append(
            send(
                b_buf.at[i, j, h], b_buf.at[ti, tj, h],
                ring_s.at[i, j, h, direction], ring_r.at[ti, tj, h], to,
            )
        )

    def got(i, j, h):
        arrived(b_buf.at[i, j, h], ring_r.at[i, j, h])

    def first_out(h):
        ring(0, 0, h, 1, 0, 0, along_first(1))
        ring(0, 0, h, 2, 0, 1, along_first(3))

    started.append(send(b_out, b_buf.at[0, 0, c], pair_s.at[0], pair_r.at[0], sibling))
    first_out(c)

    loads[2].wait()
    masks[1].wait()

    def mask_a(t, carry):
        rows = pl.ds(pl.multiple_of(t * TILE, TILE), TILE)
        for k in range(DEPTH // TILE):
            cols = pl.ds(k * TILE, TILE)
            keep = am[t, k].astype(jnp.float32)
            a_buf[c, rows, cols] = (a_buf[c, rows, cols].astype(jnp.float32) * keep).astype(jnp.bfloat16)
        return carry

    lax.fori_loop(0, ROWS // TILE, mask_a, 0)
    arrived(b_buf.at[0, 0, 1 - c], pair_r.at[0])
    first_out(1 - c)
    started.append(send(a_buf.at[c], a_buf.at[c], pair_s.at[1], pair_r.at[1], sibling))

    def first_forward(h):
        got(1 + h, 0, h)
        ring(1 + h, 0, h, 3, 0, h, along_first(1 + 2 * h))

    def second_forward(i, h):
        got(i, 1 + h, h)
        ring(i, 1 + h, h, i, 3, 2 + h, along_second(1 + 2 * h))

    def second_rest(i):
        got(i, 1, 1)
        got(i, 2, 0)

    def second_out(i, h):
        ring(i, 0, h, i, 1, 2, along_second(1))
        ring(i, 0, h, i, 2, 3, along_second(3))

    def second_both(i):
        for h in range(2):
            ring(i, 0, h, i, 1 + h, 2 + h, along_second(1 + 2 * h))
        for h in range(2):
            ring(i, 0, 1 - h, i, 1 + h, 2 + h, along_second(1 + 2 * h))

    def product(*slots, first=0, last=ROWS // BLOCK):
        def step(t, carry):
            rows = pl.ds(pl.multiple_of(t * BLOCK, BLOCK), BLOCK)
            total = None
            for h in range(2):
                units = [b_buf[i, j, h] for i, j in slots]
                unit = units[0] if len(units) == 1 else jnp.concatenate(units, axis=1)
                part = jnp.dot(a_buf[h, rows, :], unit, preferred_element_type=jnp.float32)
                total = part if total is None else total + part
            for n, (i, j) in enumerate(slots):
                c_buf[i * 4 + j, rows, :] = total[:, n * WIDE : (n + 1) * WIDE]
            return carry

        lax.fori_loop(first, last, step, 0)

    def step_of(i):
        if isinstance(i, int):
            return STEP[i]
        return jnp.where(i == 0, 0, jnp.where(i == 1, 3, i - 1))

    def place(i, j):
        di, dj = step_of(i), step_of(j)
        return (x + di * on_x + dj * on_z) % 4, (z + di * on_z + dj * on_x) % 4

    def half(n):
        return pl.ds(n * HALF, HALF)

    def pack(u, n):
        blocks = [pl.ds(t * TILE, TILE) for t in range(HALF // TILE)]
        top = jnp.full((1, WIDE), 1e-30, jnp.float32)
        for rows in blocks:
            top = jnp.maximum(top, jnp.max(jnp.abs(c_buf.at[u, half(n)][rows, :]), axis=0, keepdims=True))
        level = jnp.floor(STEPS * jnp.log2(32000.0 / top))
        scale = jnp.exp2(level / STEPS)
        for rows in blocks:
            value = jnp.floor(c_buf.at[u, half(n)][rows, :] * scale + 0.5)
            code[u, n, rows, :] = value.astype(jnp.int32).astype(jnp.int16)
        code[u, n, pl.ds(HALF, EXTRA), :] = (
            jnp.broadcast_to(level, (EXTRA, WIDE)).astype(jnp.int32).astype(jnp.int16)
        )

    def size_of(ref):
        level = ref[pl.ds(HALF, EXTRA), :].astype(jnp.int32).astype(jnp.float32)
        return jnp.exp2(-level[:1, :] / STEPS)

    def decode(ref, rows, size):
        return ref[rows, :].astype(jnp.int32).astype(jnp.float32) * size

    def y_copy(u, n, dst, ss, rs, to):
        return pltpu.make_async_remote_copy(
            src_ref=code.at[u, n], dst_ref=dst, send_sem=ss, recv_sem=rs, device_id=to, device_id_type=MESH
        )

    def far_copy(u, n, zz):
        return y_copy(u, n, near.at[n, zz], y_s.at[u, n], y_r.at[n, zz], along_y(3 if n == 0 else 1))

    def near_copy(u, n, side, zz):
        return y_copy(
            u, n, mine.at[side, zz, n], y_s.at[u, n], y_r.at[2 + side * 2 + n, zz], along_y(3 if side == 0 else 1)
        )

    def pass_on(i, j, n):
        u = i * 4 + j
        xx, zz = place(i, j)
        role = (y - xx + 4) % 4

        @pl.when(role == 2)
        def _():
            pack(u, n)
            far_copy(u, n, zz).start()

        @pl.when(role == (1 if n == 1 else 3))
        def _():
            pack(u, n)
            near_copy(u, n, 1 - n, zz).start()

    def add_on(i, j):
        u = i * 4 + j
        xx, zz = place(i, j)
        role = (y - xx + 4) % 4

        def add(n, side):
            ref = near.at[n, zz]
            arrived(ref, y_r.at[n, zz])
            size = size_of(ref)
            for t in range(HALF // TILE):
                rows = pl.ds(t * TILE, TILE)
                c_buf.at[u, half(n)][rows, :] = c_buf.at[u, half(n)][rows, :] + decode(ref, rows, size)
            pack(u, n)
            near_copy(u, n, side, zz).start()

        @pl.when(role == 1)
        def _():
            add(0, 0)

        @pl.when(role == 3)
        def _():
            add(1, 1)

    waiting = []

    def run(*slots, lag=2):
        product(*slots)
        for i, j in slots:
            for n in range(2):
                pass_on(i, j, n)
        waiting.append(slots)
        settle(lag)

    def settle(lag):
        while len(waiting) > lag:
            for i, j in waiting.pop(0):
                add_on(i, j)

    rel = (y - x + 4) % 4

    def pick(other, *by_rel):
        i = jnp.where(rel == 0, by_rel[0], jnp.where(rel == 1, by_rel[1], jnp.where(rel == 2, by_rel[2], by_rel[3])))
        return jnp.where(c == 1, other, i)

    order = [pick(0, 1, 1, 0, 2), pick(1, 3, 0, 1, 0), pick(2, 2, 3, 2, 3), pick(3, 0, 2, 3, 1)]

    def neighbours(p):
        for h in range(2):
            second_forward(order[p], h)
        second_rest(order[p])
        run((order[p], 1), (order[p], 2))

    def across(p, lag=2):
        for h in range(2):
            got(order[p], 3, h)
        run((order[p], 3), lag=lag)

    ahead = (y - x + 4) % 4
    slot = (ahead == 1) * 2 + (ahead == 2) * 3 + (ahead == 3) * 1

    def out_at(spot):
        return o_ref.at[:, pl.ds(pl.multiple_of(spot * WIDE, WIDE), WIDE)]

    def finish(p):
        u = jnp.where(c == 0, slot * 4 + p, p * 4 + slot)
        zz = (z + STEP[p]) % 4
        spot = (zz % 2) * 2 + c
        stays = zz // 2 == c

        def total(ref):
            for n in range(2):
                refs = [mine.at[side, zz, n] for side in range(2)]
                for side in range(2):
                    arrived(refs[side], y_r.at[2 + side * 2 + n, zz])
                sizes = [size_of(r) for r in refs]
                for t in range(HALF // TILE):
                    rows = pl.ds(t * TILE, TILE)
                    others = [decode(r, rows, size) for r, size in zip(refs, sizes)]
                    value = c_buf.at[u, half(n)][rows, :] + (others[0] + others[1])
                    ref[pl.ds(n * HALF + t * TILE, TILE), :] = value.astype(jnp.bfloat16)

        @pl.when(stays)
        def _():
            total(out_at(spot))

        @pl.when(jnp.logical_not(stays))
        def _():
            total(out_send.at[zz % 2])
            send(out_send.at[zz % 2], out_at(spot), o_s.at[zz % 2], o_r.at[zz % 2], sibling)

    arrived(a_buf.at[1 - c], pair_r.at[1])
    run((0, 0))
    for h in (c, 1 - c):
        first_forward(h)
        got(2 - h, 0, h)
        second_out(order[0], h)
    run((1, 0), (2, 0))
    got(3, 0, 0)
    got(3, 0, 1)
    second_both(order[1])
    run((3, 0))
    neighbours(0)
    second_both(order[2])
    neighbours(1)
    across(0)
    second_both(order[3])
    neighbours(2)
    across(1)
    neighbours(3)
    across(2, lag=0)
    for j in range(3):
        finish(j)
    for h in range(2):
        got(order[3], 3, h)
    for n in range(2):
        product((order[3], 3), first=2 * n, last=2 * n + 2)
        pass_on(order[3], 3, n)
    add_on(order[3], 3)
    finish(3)
    for n in range(2):
        arrived(out_at(n * 2 + 1 - c), o_r.at[n])

    for copy in started:
        copy.wait_send()
    for u in range(16):
        i, j = u // 4, u % 4
        xx, zz = place(i, j)
        role = (y - xx + 4) % 4

        @pl.when(role != 0)
        def _():
            for n in range(2):
                far_copy(u, n, zz).wait_send()

    for n in range(2):
        pltpu.make_async_remote_copy(
            src_ref=out_send.at[n], dst_ref=out_send.at[n], send_sem=o_s.at[n], recv_sem=o_s.at[n],
            device_id=sibling, device_id_type=MESH,
        ).wait_send()


def per_device(amplitudes, integrals, amp_mask, int_mask):
    bf16, f32 = jnp.bfloat16, jnp.float32
    dma = pltpu.SemaphoreType.DMA
    return pl.pallas_call(
        kernel,
        out_shape=jax.ShapeDtypeStruct((ROWS, 4 * WIDE), bf16),
        in_specs=[
            pl.BlockSpec(memory_space=pl.ANY),
            pl.BlockSpec(memory_space=pl.ANY),
            pl.BlockSpec(memory_space=pltpu.HBM),
            pl.BlockSpec(memory_space=pltpu.HBM),
        ],
        out_specs=pl.BlockSpec(memory_space=pltpu.VMEM),
        scratch_shapes=[
            pltpu.VMEM((2, ROWS, DEPTH), bf16),
            pltpu.VMEM((2, DEPTH, WIDE), bf16),
            pltpu.VMEM((DEPTH, WIDE), bf16),
            pltpu.VMEM((4, 4, 2, DEPTH, WIDE), bf16),
            pltpu.VMEM((16, ROWS, WIDE), f32),
            pltpu.VMEM((16, 2, HALF + EXTRA, WIDE), jnp.int16),
            pltpu.VMEM((2, 4, HALF + EXTRA, WIDE), jnp.int16),
            pltpu.VMEM((2, 4, 2, HALF + EXTRA, WIDE), jnp.int16),
            pltpu.VMEM((2, ROWS, WIDE), bf16),
            pltpu.SMEM((8, 16), jnp.int32),
            pltpu.SMEM((2, 16), jnp.int32),
            dma((5,)),
            dma((2,)),
            dma((2,)),
            dma((4, 4, 2, 4)),
            dma((4, 4, 2)),
            dma((16, 2)),
            dma((6, 4)),
            dma((2,)),
            dma((2,)),
        ],
        compiler_params=pltpu.CompilerParams(
            collective_id=0, has_side_effects=True, vmem_limit_bytes=52 << 20
        ),
    )(amplitudes, integrals, pltpu.with_memory_space_constraint(amp_mask, pltpu.HBM), pltpu.with_memory_space_constraint(int_mask.T, pltpu.HBM))


def solution(mesh):
    in_specs = (P("row", "col"), P("col", "row"), P("row", "col"), P("col", "row"))
    out_specs = P("row", "col")
    return jax.shard_map(
        per_device, mesh=mesh, in_specs=in_specs, out_specs=out_specs, check_vma=False
    )
```
